32 devices in a mesh: occ: 4 (over z), vir: 8 (over y, x, core).
Axes of the slice: x: 2, y: 2, z: 4, core: 2. Of those that a mesh axis runs over, the one named last changes fastest.
Arguments:
- amplitudes: bfloat16 [1280, 6144], P('occ', 'vir'), may hold values from -6 to 6
- ladder_tiles: bfloat16 [2304, 128, 128], P(('occ', 'vir')), may hold values from -0.078125 to 0.078125
- block_list: int32 [2304, 2], P(('occ', 'vir')), may hold values from -1 to 47, as said below
Outputs:
- residual: bfloat16 [1280, 6144], P('occ', 'vir')
The draws below stay inside these ranges and needn't reach their ends.
Inputs may be any that keep to these rules, and one draw needn't show every extreme that they name: `block_list`: rows come in runs of 72, one run a device, devices in the order occ then vir. A live row on vir index v has its out-tile among v's own tiles v * 6 to v * 6 + 5 and its in-tile among the 48 tiles of v's aligned group of 8 vir indices, both tiles of one irrep; each such equal-irrep pair stands once over the occ indices. Dead rows are -1, -1. Some vir index has all 72 rows live on every occ index.
All inputs are finite; a program needn't handle non-finite values.
Results may differ from the reference program's by a relative error of at most 0.001.
Values may be sent and summed in bfloat16 or wider, within the bound.
A program may use at most 64 MiB of HBM per device.

```python
import jax
import jax.numpy as jnp
from jax import lax

TV = 128
KT = 6
GROUP = 8
SQ = 72
NOCCP = 1280
NVP = 6144
NBLK = 2304
N_OCC = 4
N_VIR = 8


def draw_block_list(key, part):
    group_count = N_VIR // GROUP
    split_points = jax.random.randint(jax.random.fold_in(key, 11), (group_count,), 0, GROUP)
    forced = jax.random.randint(jax.random.fold_in(key, 12), (), 0, group_count)
    split_points = jnp.where(jnp.arange(group_count) == forced, 0, split_points)
    rank_keys = jax.random.split(jax.random.fold_in(key, 13), N_VIR)
    rank_perms = jax.vmap(lambda one_key: jax.random.permutation(one_key, SQ * N_OCC))(rank_keys).astype(jnp.int32)
    device_ids = jnp.arange(N_OCC * N_VIR, dtype=jnp.int32)
    occ_ids = device_ids // N_VIR
    vir_ids = device_ids % N_VIR
    group_ids = vir_ids // GROUP
    position = vir_ids % GROUP
    split_here = split_points[group_ids]
    in_lower = position < split_here
    first_device = jnp.where(in_lower, group_ids * GROUP, group_ids * GROUP + split_here)
    members = jnp.where(in_lower, split_here, GROUP - split_here)
    slot_ids = jnp.arange(SQ, dtype=jnp.int32)
    raw_rank = slot_ids[None, :] * N_OCC + occ_ids[:, None]
    block_rank = rank_perms[vir_ids[:, None], raw_rank]
    is_live = block_rank < KT * KT * members[:, None]
    out_tile = vir_ids[:, None] * KT + block_rank % KT
    in_tile = first_device[:, None] * KT + block_rank // KT
    out_tile = jnp.where(is_live, out_tile, -1)
    in_tile = jnp.where(is_live, in_tile, -1)
    return jnp.stack([in_tile, out_tile], axis=-1).reshape(N_OCC * N_VIR * SQ, 2).astype(jnp.int32)


def shard_levels(own_key, dims, cuts, smallest, largest):
    factor_of = 1.0
    for dim, parts in cuts:
        steps = jax.random.uniform(jax.random.fold_in(jax.random.fold_in(own_key, 6), dim), (parts,), jnp.float32, smallest / len(cuts), largest / len(cuts))
        factor_of = factor_of * jnp.repeat(jnp.exp(steps), dims[dim] // parts).reshape((-1,) + (1,) * (len(dims) - 1 - dim))
    return factor_of


def centred(stream_key, shape, deviation, most, cuts=(), kind=jnp.bfloat16):
    factor_of = shard_levels(stream_key, shape, cuts, -0.22, 0.18) if cuts else 1.0
    array = jax.random.normal(stream_key, shape, jnp.float32) * deviation * factor_of
    return jnp.minimum(jnp.maximum(array, -most), most).astype(kind)


def setup_inputs(seed: int = 0) -> dict:
    arg_keys = jax.random.split(jax.random.key(seed), 4)
    amplitudes = centred(arg_keys[0], (NOCCP, NVP), 1.0, 6.0, ((0, 4), (1, 8)))
    ladder_tiles = centred(arg_keys[1], (NBLK, TV, TV), (TV * KT * GROUP) ** -0.5, 0.078125, ((0, 32),))
    block_list = draw_block_list(jax.random.fold_in(arg_keys[3], 71), 0)
    return {"amplitudes": amplitudes, "ladder_tiles": ladder_tiles, "block_list": block_list}


def reference(amplitudes, ladder_tiles, block_list):
    tile_count = amplitudes.shape[1] // TV
    tiles_by_col = amplitudes.reshape(NOCCP, tile_count, TV)
    block_lists = block_list.reshape(N_OCC, N_VIR, SQ, 2)
    ladder_mats = ladder_tiles.reshape(N_OCC, N_VIR, SQ, TV, TV)

    def column(vir_index):
        entries = lax.dynamic_index_in_dim(block_lists, vir_index, 1, keepdims=False).reshape(N_OCC * SQ, 2)
        tile_mats = lax.dynamic_index_in_dim(ladder_mats, vir_index, 1, keepdims=False).reshape(N_OCC * SQ, TV, TV)
        in_tile = jnp.clip(entries[:, 0], 0, tile_count - 1).astype(jnp.int32)
        out_tile = entries[:, 1] - vir_index * KT
        picker = (out_tile[:, None] == jnp.arange(KT, dtype=jnp.int32)[None, :]).astype(jnp.float32)
        taken_cols = jnp.take(tiles_by_col, in_tile, axis=1).astype(jnp.float32)
        contrib = jnp.einsum("psk,skn->psn", taken_cols, tile_mats.astype(jnp.float32), precision=lax.Precision.HIGHEST)
        return jnp.einsum("psn,sa->pan", contrib, picker, precision=lax.Precision.HIGHEST)

    columns_out = lax.map(column, jnp.arange(N_VIR, dtype=jnp.int32))
    ladder = columns_out.transpose(1, 0, 2, 3).reshape(NOCCP, N_VIR * KT * TV)
    return ladder.astype(jnp.bfloat16)
```

```python
import jax
import jax.numpy as jnp
from jax import lax
from jax.experimental import pallas as pl
from jax.experimental.pallas import tpu as pltpu
from jax.sharding import PartitionSpec as P

TV = 128
GROUP = 8


def from_partner(block, axis, apart):
    count = lax.axis_size(axis)
    route = []
    for low in range(count):
        high = low | 1 << apart
        if high != low and high < count:
            route += [(low, high), (high, low)]
    return lax.ppermute(block, axis, route)


def collect_group(local_amps, vir_index):
    gathered = local_amps
    for bit_number in range(GROUP.bit_length() - 1):
        partner = from_partner(gathered, "vir", bit_number)
        is_low = vir_index >> bit_number & 1 == 0
        gathered = jnp.where(
            is_low,
            jnp.concatenate([gathered, partner], axis=1),
            jnp.concatenate([partner, gathered], axis=1),
        )
    return gathered


def ladder_block(group_amps, ladder_mats, block_pairs, vir_index, tiles_here):
    group_count = group_amps.shape[1] // TV
    first_tile = vir_index // GROUP * GROUP * tiles_here
    out_tile = block_pairs[:, 1] - vir_index * tiles_here
    in_tile = block_pairs[:, 0] - first_tile
    is_live = block_pairs[:, 1] >= 0
    pair_index = jnp.where(is_live, in_tile * tiles_here + out_tile, -1)
    slot_onehot = (
        pair_index[:, None] == jnp.arange(group_count * tiles_here, dtype=jnp.int32)[None, :]
    ).astype(jnp.bfloat16)
    placed = jnp.einsum(
        "sp,skn->pkn", slot_onehot, ladder_mats, preferred_element_type=jnp.float32
    ).astype(jnp.bfloat16)
    dense_weight = (
        placed.reshape(group_count, tiles_here, TV, TV)
        .transpose(0, 2, 1, 3)
        .reshape(group_count * TV, tiles_here * TV)
    )
    return jnp.dot(group_amps, dense_weight, preferred_element_type=jnp.float32)


def tiles_travel(amplitudes, ladder_tiles, block_list):
    tiles_here = amplitudes.shape[1] // TV
    vir_index = lax.axis_index("vir")
    all_tiles, all_pairs = (
        lax.all_gather(ladder_tiles, "occ", axis=0, tiled=True),
        lax.all_gather(block_list, "occ", axis=0, tiled=True),
    )
    group_amps = collect_group(amplitudes, vir_index)
    residual = ladder_block(group_amps, all_tiles, all_pairs, vir_index, tiles_here).astype(
        jnp.bfloat16
    )
    return residual


def place_body(in_ref, out_ref, tiles_ref, dense_ref):
    def clear(k, carry):
        rows = pl.ds(pl.multiple_of(k * TV, TV), TV)
        dense_ref[rows, :] = jnp.zeros((TV, dense_ref.shape[1]), dense_ref.dtype)
        return carry

    lax.fori_loop(0, dense_ref.shape[0] // TV, clear, 0)

    def put(slot, carry):
        @pl.when(out_ref[slot] >= 0)
        def _():
            rows = pl.ds(pl.multiple_of(in_ref[slot] * TV, TV), TV)
            cols = pl.ds(pl.multiple_of(out_ref[slot] * TV, TV), TV)
            dense_ref[rows, cols] = tiles_ref[slot]

        return carry

    lax.fori_loop(0, tiles_ref.shape[0], put, 0)


def place_tiles(ladder_tiles, block_pairs, tiles_here):
    vir_index = lax.axis_index("vir")
    is_live = block_pairs[:, 1] >= 0
    in_tile = block_pairs[:, 0] - vir_index // GROUP * GROUP * tiles_here
    out_tile = block_pairs[:, 1] - vir_index * tiles_here
    in_tile = jnp.where(is_live, jnp.clip(in_tile, 0, GROUP * tiles_here - 1), 0)
    out_tile = jnp.where(is_live, jnp.clip(out_tile, 0, tiles_here - 1), -1)
    return pl.pallas_call(
        place_body,
        out_shape=jax.ShapeDtypeStruct((GROUP * tiles_here * TV, tiles_here * TV), ladder_tiles.dtype),
        in_specs=[
            pl.BlockSpec(memory_space=pltpu.SMEM),
            pl.BlockSpec(memory_space=pltpu.SMEM),
            pl.BlockSpec(memory_space=pltpu.VMEM),
        ],
        out_specs=pl.BlockSpec(memory_space=pltpu.VMEM),
        compiler_params=pltpu.CompilerParams(vmem_limit_bytes=32 << 20),
        cost_estimate=pl.CostEstimate(flops=0, bytes_accessed=24 << 20, transcendentals=0),
        name="place_tiles",
    )(in_tile, out_tile, ladder_tiles)


ORDER = (0, 1, 3, 2)
N_SEM = 52


def ladder_body(amps_ref, dense_ref, out_ref, all_ref, part, near, far, send_sems, recv_sems):
    o, v = lax.axis_index("occ"), lax.axis_index("vir")
    y, x, c = v // 4, v // 2 % 2, v % 2
    v_x = y * 4 + (1 - x) * 2 + c
    v_y = (1 - y) * 4 + x * 2 + c
    v_xy = (1 - y) * 4 + (1 - x) * 2 + c
    v_c = y * 4 + x * 2 + 1 - c
    o_1 = o + 1 - 2 * (o % 2)
    o_of = (o, o_1, (o + 2) % 4, (o_1 + 2) % 4)
    rows, width = amps_ref.shape
    half = rows // 2
    whole, top, low = pl.ds(0, rows), pl.ds(0, half), pl.ds(half, half)

    barrier = pltpu.get_barrier_semaphore()
    peers = [(o_of[1], v), (o_of[2], v), (o_of[3], v), (o, v_x), (o, v_y), (o, v_c)]
    for peer in peers:
        pl.semaphore_signal(barrier, inc=1, device_id=peer, device_id_type=pl.DeviceIdType.MESH)
    all_ref[o, v] = amps_ref[...]
    pl.semaphore_wait(barrier, len(peers))

    started = []

    def move(src, dst, number, peer):
        copy = pltpu.make_async_remote_copy(
            src_ref=src,
            dst_ref=dst,
            send_sem=send_sems.at[number],
            recv_sem=recv_sems.at[number],
            device_id=peer,
            device_id_type=pl.DeviceIdType.MESH,
        )
        return copy

    def send(block, tile, span, number, peer):
        ref = all_ref.at[block, tile, span]
        copy = move(ref, ref, number, peer)
        copy.start()
        started.append(copy)

    def arrived(block, tile, span, number, peer):
        ref = all_ref.at[block, tile, span]
        move(ref, ref, number, peer).wait_recv()

    for e in (1, 3, 2):
        send(o, v, whole, e, (o_of[e], v))

    def own_stage(k):
        block, base = o_of[ORDER[k]], 4 + 11 * k
        if k > 0:
            arrived(block, v, whole, ORDER[k], (block, v))
        send(block, v, top, base, (o, v_x))
        send(block, v, low, base + 1, (o, v_y))
        send(block, v, low, base + 2, (o, v_x))
        send(block, v, top, base + 3, (o, v_y))
        send(block, v, whole, base + 6, (o, v_c))

    def forward_stage(k):
        block, base = o_of[ORDER[k]], 4 + 11 * k
        arrived(block, v_x, top, base, (o, v_x))
        send(block, v_x, top, base + 4, (o, v_y))
        arrived(block, v_y, low, base + 1, (o, v_y))
        send(block, v_y, low, base + 5, (o, v_x))
        arrived(block, v_x, low, base + 2, (o, v_x))
        send(block, v_x, whole, base + 7, (o, v_c))
        arrived(block, v_y, top, base + 3, (o, v_y))
        send(block, v_y, whole, base + 8, (o, v_c))

    def corner_stage(k):
        block, base = o_of[ORDER[k]], 4 + 11 * k
        arrived(block, v_xy, top, base + 4, (o, v_y))
        send(block, v_xy, top, base + 9, (o, v_c))
        arrived(block, v_xy, low, base + 5, (o, v_x))
        send(block, v_xy, low, base + 10, (o, v_c))

    def other_core(tile):
        return tile + 1 - 2 * c

    def product_stage(k):
        e = ORDER[k]
        block, base = o_of[e], 4 + 11 * k
        arrived(block, other_core(v), whole, base + 6, (o, v_c))
        arrived(block, other_core(v_x), whole, base + 7, (o, v_c))
        arrived(block, other_core(v_y), whole, base + 8, (o, v_c))
        arrived(block, other_core(v_xy), top, base + 9, (o, v_c))
        arrived(block, other_core(v_xy), low, base + 10, (o, v_c))

        def term(tile):
            inner = pl.ds(pl.multiple_of(tile * width, TV), width)
            return jnp.dot(
                all_ref[block, tile], dense_ref[inner, :], preferred_element_type=jnp.float32
            )

        part[e] = jnp.zeros(part.shape[1:], jnp.float32)

        def add(tile, carry):
            part[e] += term(tile)
            return carry

        lax.fori_loop(0, GROUP, add, 0)
        if e == 1 or e == 3:
            slot = e // 2
            copy = move(part.at[e], near.at[slot], 48 + slot, (o_of[1], v))
            copy.start()
            started.append(copy)
        if e == 2:
            move(part.at[2], near.at[1], 49, (o_of[1], v)).wait_recv()
            part[2] += near[1]
            copy = move(part.at[2], far, 50, (o_of[2], v))
            copy.start()
            started.append(copy)

    for step in range(len(ORDER) + 3):
        for lag, stage in enumerate((own_stage, forward_stage, corner_stage, product_stage)):
            if 0 <= step - lag < len(ORDER):
                stage(step - lag)

    move(part.at[0], near.at[0], 48, (o_of[1], v)).wait_recv()
    move(part.at[0], far, 50, (o_of[2], v)).wait_recv()
    out_ref[...] = (part[0] + near[0] + far[...]).astype(out_ref.dtype)
    for copy in started:
        copy.wait_send()


def tiles_stay(amplitudes, ladder_tiles, block_list):
    tiles_here = amplitudes.shape[1] // TV
    n_occ, n_vir = lax.axis_size("occ"), lax.axis_size("vir")
    dense = place_tiles(ladder_tiles, block_list, tiles_here)
    rows, width = amplitudes.shape
    return pl.pallas_call(
        ladder_body,
        out_shape=jax.ShapeDtypeStruct((rows, width), jnp.bfloat16),
        in_specs=[pl.BlockSpec(memory_space=pltpu.VMEM)] * 2,
        out_specs=pl.BlockSpec(memory_space=pltpu.VMEM),
        scratch_shapes=[
            pltpu.VMEM((n_occ, n_vir, rows, width), jnp.bfloat16),
            pltpu.VMEM((n_occ, rows, width), jnp.float32),
            pltpu.VMEM((2, rows, width), jnp.float32),
            pltpu.VMEM((rows, width), jnp.float32),
            pltpu.SemaphoreType.DMA((N_SEM,)),
            pltpu.SemaphoreType.DMA((N_SEM,)),
        ],
        compiler_params=pltpu.CompilerParams(
            collective_id=0, has_side_effects=True, vmem_limit_bytes=48 << 20
        ),
        name="ladder",
    )(amplitudes, dense)


def per_device(amplitudes, ladder_tiles, block_list):
    everywhere = lax.axis_size("occ") * amplitudes.size * GROUP * 2
    if lax.axis_size("vir") == GROUP and lax.axis_size("occ") == 4 and everywhere <= 16 << 20:
        return tiles_stay(amplitudes, ladder_tiles, block_list)
    return tiles_travel(amplitudes, ladder_tiles, block_list)


def solution(mesh):
    return jax.shard_map(
        per_device,
        mesh=mesh,
        in_specs=(P("occ", "vir"), P(("occ", "vir"), None, None), P(("occ", "vir"), None)),
        out_specs=P("occ", "vir"),
        check_vma=False,
    )
```

```python
import jax
import jax.numpy as jnp
from jax import lax
from jax.experimental import pallas as pl
from jax.experimental.pallas import tpu as pltpu
from jax.sharding import PartitionSpec as P

TV = 128
GROUP = 8


def from_partner(block, axis, apart):
    count = lax.axis_size(axis)
    route = []
    for low in range(count):
        high = low | 1 << apart
        if high != low and high < count:
            route += [(low, high), (high, low)]
    return lax.ppermute(block, axis, route)


def collect_group(local_amps, vir_index):
    gathered = local_amps
    for bit_number in range(GROUP.bit_length() - 1):
        partner = from_partner(gathered, "vir", bit_number)
        is_low = vir_index >> bit_number & 1 == 0
        gathered = jnp.where(
            is_low,
            jnp.concatenate([gathered, partner], axis=1),
            jnp.concatenate([partner, gathered], axis=1),
        )
    return gathered


def ladder_block(group_amps, ladder_mats, block_pairs, vir_index, tiles_here):
    group_count = group_amps.shape[1] // TV
    first_tile = vir_index // GROUP * GROUP * tiles_here
    out_tile = block_pairs[:, 1] - vir_index * tiles_here
    in_tile = block_pairs[:, 0] - first_tile
    is_live = block_pairs[:, 1] >= 0
    pair_index = jnp.where(is_live, in_tile * tiles_here + out_tile, -1)
    slot_onehot = (
        pair_index[:, None] == jnp.arange(group_count * tiles_here, dtype=jnp.int32)[None, :]
    ).astype(jnp.bfloat16)
    placed = jnp.einsum(
        "sp,skn->pkn", slot_onehot, ladder_mats, preferred_element_type=jnp.float32
    ).astype(jnp.bfloat16)
    dense_weight = (
        placed.reshape(group_count, tiles_here, TV, TV)
        .transpose(0, 2, 1, 3)
        .reshape(group_count * TV, tiles_here * TV)
    )
    return jnp.dot(group_amps, dense_weight, preferred_element_type=jnp.float32)


def tiles_travel(amplitudes, ladder_tiles, block_list):
    tiles_here = amplitudes.shape[1] // TV
    vir_index = lax.axis_index("vir")
    all_tiles, all_pairs = (
        lax.all_gather(ladder_tiles, "occ", axis=0, tiled=True),
        lax.all_gather(block_list, "occ", axis=0, tiled=True),
    )
    group_amps = collect_group(amplitudes, vir_index)
    residual = ladder_block(group_amps, all_tiles, all_pairs, vir_index, tiles_here).astype(
        jnp.bfloat16
    )
    return residual


def place_body(in_ref, out_ref, tiles_ref, dense_ref):
    def clear(k, carry):
        rows = pl.ds(pl.multiple_of(k * TV, TV), TV)
        dense_ref[rows, :] = jnp.zeros((TV, dense_ref.shape[1]), dense_ref.dtype)
        return carry

    lax.fori_loop(0, dense_ref.shape[0] // TV, clear, 0)

    def put(slot, carry):
        @pl.when(out_ref[slot] >= 0)
        def _():
            rows = pl.ds(pl.multiple_of(in_ref[slot] * TV, TV), TV)
            cols = pl.ds(pl.multiple_of(out_ref[slot] * TV, TV), TV)
            dense_ref[rows, cols] = tiles_ref[slot]

        return carry

    lax.fori_loop(0, tiles_ref.shape[0], put, 0)


def place_tiles(ladder_tiles, block_pairs, tiles_here):
    vir_index = lax.axis_index("vir")
    is_live = block_pairs[:, 1] >= 0
    in_tile = block_pairs[:, 0] - vir_index // GROUP * GROUP * tiles_here
    out_tile = block_pairs[:, 1] - vir_index * tiles_here
    in_tile = jnp.where(is_live, jnp.clip(in_tile, 0, GROUP * tiles_here - 1), 0)
    out_tile = jnp.where(is_live, jnp.clip(out_tile, 0, tiles_here - 1), -1)
    return pl.pallas_call(
        place_body,
        out_shape=jax.ShapeDtypeStruct((GROUP * tiles_here * TV, tiles_here * TV), ladder_tiles.dtype),
        in_specs=[
            pl.BlockSpec(memory_space=pltpu.SMEM),
            pl.BlockSpec(memory_space=pltpu.SMEM),
            pl.BlockSpec(memory_space=pltpu.VMEM),
        ],
        out_specs=pl.BlockSpec(memory_space=pltpu.VMEM),
        compiler_params=pltpu.CompilerParams(vmem_limit_bytes=32 << 20),
        cost_estimate=pl.CostEstimate(flops=0, bytes_accessed=24 << 20, transcendentals=0),
        name="place_tiles",
    )(in_tile, out_tile, ladder_tiles)


N_SEM = 52


def ladder_body(
    amps_ref, dense_hbm, out_ref, dense_ref, all_ref, part, near, far, send_sems, recv_sems, dense_sem
):
    o, v = lax.axis_index("occ"), lax.axis_index("vir")
    y, x, c = v // 4, v // 2 % 2, v % 2
    v_x = y * 4 + (1 - x) * 2 + c
    v_y = (1 - y) * 4 + x * 2 + c
    v_xy = (1 - y) * 4 + (1 - x) * 2 + c
    v_c = y * 4 + x * 2 + 1 - c
    o_1 = o + 1 - 2 * (o % 2)
    o_of = (o, o_1, (o + 2) % 4, (o_1 + 2) % 4)
    rows, width = amps_ref.shape
    half = rows // 2
    whole, top, low = pl.ds(0, rows), pl.ds(0, half), pl.ds(half, half)

    barrier = pltpu.get_barrier_semaphore()
    peers = [(o_of[1], v), (o_of[2], v), (o_of[3], v), (o, v_x), (o, v_y), (o, v_c)]
    for peer in peers:
        pl.semaphore_signal(barrier, inc=1, device_id=peer, device_id_type=pl.DeviceIdType.MESH)
    all_ref[o, v] = amps_ref[...]
    pl.semaphore_wait(barrier, len(peers))

    started = []

    def move(src, dst, number, peer):
        copy = pltpu.make_async_remote_copy(
            src_ref=src,
            dst_ref=dst,
            send_sem=send_sems.at[number],
            recv_sem=recv_sems.at[number],
            device_id=peer,
            device_id_type=pl.DeviceIdType.MESH,
        )
        return copy

    def send(block, tile, span, number, peer):
        ref = all_ref.at[block, tile, span]
        copy = move(ref, ref, number, peer)
        copy.start()
        started.append(copy)

    def arrived(block, tile, span, number, peer):
        ref = all_ref.at[block, tile, span]
        move(ref, ref, number, peer).wait_recv()

    fetch = pltpu.make_async_copy(dense_hbm, dense_ref, dense_sem)
    fetch.start()

    def row_stage(e):
        send(o, v, whole, e, (o_of[e], v))

    def own_stage(e):
        block, base = o_of[e], 4 + 11 * e
        if e > 0:
            arrived(block, v, whole, e, (block, v))
        send(block, v, top, base, (o, v_x))
        send(block, v, low, base + 1, (o, v_y))
        send(block, v, low, base + 2, (o, v_x))
        send(block, v, top, base + 3, (o, v_y))
        send(block, v, whole, base + 6, (o, v_c))

    def forward_stage(e):
        block, base = o_of[e], 4 + 11 * e
        arrived(block, v_x, top, base, (o, v_x))
        send(block, v_x, top, base + 4, (o, v_y))
        arrived(block, v_y, low, base + 1, (o, v_y))
        send(block, v_y, low, base + 5, (o, v_x))
        arrived(block, v_x, low, base + 2, (o, v_x))
        send(block, v_x, whole, base + 7, (o, v_c))
        arrived(block, v_y, top, base + 3, (o, v_y))
        send(block, v_y, whole, base + 8, (o, v_c))

    def corner_stage(e):
        block, base = o_of[e], 4 + 11 * e
        arrived(block, v_xy, top, base + 4, (o, v_y))
        send(block, v_xy, top, base + 9, (o, v_c))
        arrived(block, v_xy, low, base + 5, (o, v_x))
        send(block, v_xy, low, base + 10, (o, v_c))

    def other_core(tile):
        return tile + 1 - 2 * c

    def product_stage(e):
        block, base = o_of[e], 4 + 11 * e
        arrived(block, other_core(v), whole, base + 6, (o, v_c))
        arrived(block, other_core(v_x), whole, base + 7, (o, v_c))
        arrived(block, other_core(v_y), whole, base + 8, (o, v_c))
        arrived(block, other_core(v_xy), top, base + 9, (o, v_c))
        arrived(block, other_core(v_xy), low, base + 10, (o, v_c))

        def term(tile):
            inner = pl.ds(pl.multiple_of(tile * width, TV), width)
            return jnp.dot(
                all_ref[block, tile], dense_ref[inner, :], preferred_element_type=jnp.float32
            )

        part[e] = jnp.zeros(part.shape[1:], jnp.float32)

        def add(tile, carry):
            part[e] += term(tile)
            return carry

        lax.fori_loop(0, GROUP, add, 0)
        if e == 1 or e == 3:
            slot = e // 2
            copy = move(part.at[e], near.at[slot], 48 + slot, (o_of[1], v))
            copy.start()
            started.append(copy)

    def far_stage():
        move(part.at[2], near.at[1], 49, (o_of[1], v)).wait_recv()
        part[2] += near[1]
        copy = move(part.at[2], far, 50, (o_of[2], v))
        copy.start()
        started.append(copy)

    row_stage(3)
    own_stage(0)
    forward_stage(0)
    row_stage(2)
    own_stage(3)
    row_stage(1)
    corner_stage(0)
    forward_stage(3)
    own_stage(2)
    corner_stage(3)
    fetch.wait()
    product_stage(3)
    forward_stage(2)
    corner_stage(2)
    own_stage(1)
    product_stage(2)
    product_stage(0)
    far_stage()
    forward_stage(1)
    corner_stage(1)
    product_stage(1)
    move(part.at[0], near.at[0], 48, (o_of[1], v)).wait_recv()
    move(part.at[0], far, 50, (o_of[2], v)).wait_recv()
    out_ref[...] = (part[0] + near[0] + far[...]).astype(out_ref.dtype)
    for copy in started:
        copy.wait_send()


def tiles_stay(amplitudes, ladder_tiles, block_list):
    tiles_here = amplitudes.shape[1] // TV
    n_occ, n_vir = lax.axis_size("occ"), lax.axis_size("vir")
    dense = place_tiles(ladder_tiles, block_list, tiles_here)
    rows, width = amplitudes.shape
    return pl.pallas_call(
        ladder_body,
        out_shape=jax.ShapeDtypeStruct((rows, width), jnp.bfloat16),
        in_specs=[pl.BlockSpec(memory_space=pltpu.VMEM), pl.BlockSpec(memory_space=pl.ANY)],
        out_specs=pl.BlockSpec(memory_space=pltpu.VMEM),
        scratch_shapes=[
            pltpu.VMEM(dense.shape, dense.dtype),
            pltpu.VMEM((n_occ, n_vir, rows, width), jnp.bfloat16),
            pltpu.VMEM((n_occ, rows, width), jnp.float32),
            pltpu.VMEM((2, rows, width), jnp.float32),
            pltpu.VMEM((rows, width), jnp.float32),
            pltpu.SemaphoreType.DMA((N_SEM,)),
            pltpu.SemaphoreType.DMA((N_SEM,)),
            pltpu.SemaphoreType.DMA(()),
        ],
        compiler_params=pltpu.CompilerParams(
            collective_id=0, has_side_effects=True, vmem_limit_bytes=48 << 20
        ),
        name="ladder",
    )(amplitudes, dense)


def per_device(amplitudes, ladder_tiles, block_list):
    everywhere = lax.axis_size("occ") * amplitudes.size * GROUP * 2
    if lax.axis_size("vir") == GROUP and lax.axis_size("occ") == 4 and everywhere <= 16 << 20:
        return tiles_stay(amplitudes, ladder_tiles, block_list)
    return tiles_travel(amplitudes, ladder_tiles, block_list)


def solution(mesh):
    return jax.shard_map(
        per_device,
        mesh=mesh,
        in_specs=(P("occ", "vir"), P(("occ", "vir"), None, None), P(("occ", "vir"), None)),
        out_specs=P("occ", "vir"),
        check_vma=False,
    )
```

```python
import jax
import jax.numpy as jnp
from jax import lax
from jax.experimental import pallas as pl
from jax.experimental.pallas import tpu as pltpu
from jax.sharding import PartitionSpec as P

TV = 128
GROUP = 8


def from_partner(block, axis, apart):
    count = lax.axis_size(axis)
    route = []
    for low in range(count):
        high = low | 1 << apart
        if high != low and high < count:
            route += [(low, high), (high, low)]
    return lax.ppermute(block, axis, route)


def collect_group(local_amps, vir_index):
    gathered = local_amps
    for bit_number in range(GROUP.bit_length() - 1):
        partner = from_partner(gathered, "vir", bit_number)
        is_low = vir_index >> bit_number & 1 == 0
        gathered = jnp.where(
            is_low,
            jnp.concatenate([gathered, partner], axis=1),
            jnp.concatenate([partner, gathered], axis=1),
        )
    return gathered


def ladder_block(group_amps, ladder_mats, block_pairs, vir_index, tiles_here):
    group_count = group_amps.shape[1] // TV
    first_tile = vir_index // GROUP * GROUP * tiles_here
    out_tile = block_pairs[:, 1] - vir_index * tiles_here
    in_tile = block_pairs[:, 0] - first_tile
    is_live = block_pairs[:, 1] >= 0
    pair_index = jnp.where(is_live, in_tile * tiles_here + out_tile, -1)
    slot_onehot = (
        pair_index[:, None] == jnp.arange(group_count * tiles_here, dtype=jnp.int32)[None, :]
    ).astype(jnp.bfloat16)
    placed = jnp.einsum(
        "sp,skn->pkn", slot_onehot, ladder_mats, preferred_element_type=jnp.float32
    ).astype(jnp.bfloat16)
    dense_weight = (
        placed.reshape(group_count, tiles_here, TV, TV)
        .transpose(0, 2, 1, 3)
        .reshape(group_count * TV, tiles_here * TV)
    )
    return jnp.dot(group_amps, dense_weight, preferred_element_type=jnp.float32)


def tiles_travel(amplitudes, ladder_tiles, block_list):
    tiles_here = amplitudes.shape[1] // TV
    vir_index = lax.axis_index("vir")
    all_tiles, all_pairs = (
        lax.all_gather(ladder_tiles, "occ", axis=0, tiled=True),
        lax.all_gather(block_list, "occ", axis=0, tiled=True),
    )
    group_amps = collect_group(amplitudes, vir_index)
    residual = ladder_block(group_amps, all_tiles, all_pairs, vir_index, tiles_here).astype(
        jnp.bfloat16
    )
    return residual


def place_body(in_ref, out_ref, tiles_ref, dense_ref):
    def clear(k, carry):
        rows = pl.ds(pl.multiple_of(k * TV, TV), TV)
        dense_ref[rows, :] = jnp.zeros((TV, dense_ref.shape[1]), dense_ref.dtype)
        return carry

    lax.fori_loop(0, dense_ref.shape[0] // TV, clear, 0)

    def put(slot, carry):
        @pl.when(out_ref[slot] >= 0)
        def _():
            rows = pl.ds(pl.multiple_of(in_ref[slot] * TV, TV), TV)
            cols = pl.ds(pl.multiple_of(out_ref[slot] * TV, TV), TV)
            dense_ref[rows, cols] = tiles_ref[slot]

        return carry

    lax.fori_loop(0, tiles_ref.shape[0], put, 0)


def place_tiles(ladder_tiles, block_pairs, tiles_here):
    vir_index = lax.axis_index("vir")
    is_live = block_pairs[:, 1] >= 0
    in_tile = block_pairs[:, 0] - vir_index // GROUP * GROUP * tiles_here
    out_tile = block_pairs[:, 1] - vir_index * tiles_here
    in_tile = jnp.where(is_live, jnp.clip(in_tile, 0, GROUP * tiles_here - 1), 0)
    out_tile = jnp.where(is_live, jnp.clip(out_tile, 0, tiles_here - 1), -1)
    return pl.pallas_call(
        place_body,
        out_shape=jax.ShapeDtypeStruct((GROUP * tiles_here * TV, tiles_here * TV), ladder_tiles.dtype),
        in_specs=[
            pl.BlockSpec(memory_space=pltpu.SMEM),
            pl.BlockSpec(memory_space=pltpu.SMEM),
            pl.BlockSpec(memory_space=pltpu.VMEM),
        ],
        out_specs=pl.BlockSpec(memory_space=pltpu.VMEM),
        compiler_params=pltpu.CompilerParams(vmem_limit_bytes=32 << 20),
        cost_estimate=pl.CostEstimate(flops=0, bytes_accessed=24 << 20, transcendentals=0),
        name="place_tiles",
    )(in_tile, out_tile, ladder_tiles)


N_SEM = 57
CUT = 256


def ladder_body(
    amps_ref, dense_hbm, out_ref, dense_ref, all_ref, part, near, far, send_sems, recv_sems, dense_sem
):
    o, v = lax.axis_index("occ"), lax.axis_index("vir")
    y, x, c = v // 4, v // 2 % 2, v % 2
    v_x = y * 4 + (1 - x) * 2 + c
    v_y = (1 - y) * 4 + x * 2 + c
    v_xy = (1 - y) * 4 + (1 - x) * 2 + c
    v_c = y * 4 + x * 2 + 1 - c
    o_1 = o + 1 - 2 * (o % 2)
    o_of = (o, o_1, (o + 2) % 4, (o_1 + 2) % 4)
    rows, width = amps_ref.shape
    half = rows // 2
    whole, top, low = pl.ds(0, rows), pl.ds(0, half), pl.ds(half, half)

    barrier = pltpu.get_barrier_semaphore()
    peers = [(o_of[1], v), (o_of[2], v), (o_of[3], v), (o, v_x), (o, v_y), (o, v_c)]
    for peer in peers:
        pl.semaphore_signal(barrier, inc=1, device_id=peer, device_id_type=pl.DeviceIdType.MESH)
    all_ref[o, v] = amps_ref[...]
    pl.semaphore_wait(barrier, len(peers))

    started = []

    def move(src, dst, number, peer):
        copy = pltpu.make_async_remote_copy(
            src_ref=src,
            dst_ref=dst,
            send_sem=send_sems.at[number],
            recv_sem=recv_sems.at[number],
            device_id=peer,
            device_id_type=pl.DeviceIdType.MESH,
        )
        return copy

    def send(block, tile, span, number, peer):
        ref = all_ref.at[block, tile, span]
        copy = move(ref, ref, number, peer)
        copy.start()
        started.append(copy)

    def arrived(block, tile, span, number, peer):
        ref = all_ref.at[block, tile, span]
        move(ref, ref, number, peer).wait_recv()

    fetch = pltpu.make_async_copy(dense_hbm, dense_ref, dense_sem)
    fetch.start()

    def row_stage(e):
        send(o, v, whole, e, (o_of[e], v))

    def own_stage(e):
        block, base = o_of[e], 4 + 11 * e
        if e > 0:
            arrived(block, v, whole, e, (block, v))
        send(block, v, top, base, (o, v_x))
        send(block, v, low, base + 1, (o, v_y))
        send(block, v, low, base + 2, (o, v_x))
        send(block, v, top, base + 3, (o, v_y))
        send(block, v, whole, base + 6, (o, v_c))

    def forward_stage(e):
        block, base = o_of[e], 4 + 11 * e
        arrived(block, v_x, top, base, (o, v_x))
        send(block, v_x, top, base + 4, (o, v_y))
        arrived(block, v_y, low, base + 1, (o, v_y))
        send(block, v_y, low, base + 5, (o, v_x))
        arrived(block, v_x, low, base + 2, (o, v_x))
        send(block, v_x, whole, base + 7, (o, v_c))
        arrived(block, v_y, top, base + 3, (o, v_y))
        send(block, v_y, whole, base + 8, (o, v_c))

    def corner_stage(e):
        block, base = o_of[e], 4 + 11 * e
        arrived(block, v_xy, top, base + 4, (o, v_y))
        send(block, v_xy, top, base + 9, (o, v_c))
        arrived(block, v_xy, low, base + 5, (o, v_x))
        send(block, v_xy, low, base + 10, (o, v_c))

    def other_core(tile):
        return tile + 1 - 2 * c

    def product_stage(e):
        block, base = o_of[e], 4 + 11 * e
        arrived(block, other_core(v), whole, base + 6, (o, v_c))
        arrived(block, other_core(v_x), whole, base + 7, (o, v_c))
        arrived(block, other_core(v_y), whole, base + 8, (o, v_c))
        arrived(block, other_core(v_xy), top, base + 9, (o, v_c))
        arrived(block, other_core(v_xy), low, base + 10, (o, v_c))

        for n in range(width // CUT):
            columns = pl.ds(n * CUT, CUT)
            total = None
            for tile in range(GROUP):
                term = jnp.dot(
                    all_ref[block, tile],
                    dense_ref[pl.ds(tile * width, width), columns],
                    preferred_element_type=jnp.float32,
                )
                total = term if total is None else total + term
            part[e, n] = total
            if e == 1 or e == 3:
                slot = e // 2
                copy = move(part.at[e, n], near.at[slot, n], 48 + 3 * slot + n, (o_of[1], v))
                copy.start()
                started.append(copy)

    def far_stage():
        for n in range(width // CUT):
            move(part.at[2, n], near.at[1, n], 51 + n, (o_of[1], v)).wait_recv()
            part[2, n] += near[1, n]
            copy = move(part.at[2, n], far.at[n], 54 + n, (o_of[2], v))
            copy.start()
            started.append(copy)

    row_stage(3)
    own_stage(0)
    forward_stage(0)
    row_stage(2)
    own_stage(3)
    row_stage(1)
    corner_stage(0)
    forward_stage(3)
    own_stage(2)
    corner_stage(3)
    fetch.wait()
    product_stage(3)
    forward_stage(2)
    corner_stage(2)
    own_stage(1)
    product_stage(2)
    far_stage()
    forward_stage(1)
    corner_stage(1)
    product_stage(1)
    product_stage(0)
    for n in range(width // CUT):
        move(part.at[0, n], near.at[0, n], 48 + n, (o_of[1], v)).wait_recv()
        move(part.at[0, n], far.at[n], 54 + n, (o_of[2], v)).wait_recv()
        out_ref[:, pl.ds(n * CUT, CUT)] = (part[0, n] + near[0, n] + far[n]).astype(out_ref.dtype)
    for copy in started:
        copy.wait_send()


def tiles_stay(amplitudes, ladder_tiles, block_list):
    tiles_here = amplitudes.shape[1] // TV
    n_occ, n_vir = lax.axis_size("occ"), lax.axis_size("vir")
    dense = place_tiles(ladder_tiles, block_list, tiles_here)
    rows, width = amplitudes.shape
    return pl.pallas_call(
        ladder_body,
        out_shape=jax.ShapeDtypeStruct((rows, width), jnp.bfloat16),
        in_specs=[pl.BlockSpec(memory_space=pltpu.VMEM), pl.BlockSpec(memory_space=pl.ANY)],
        out_specs=pl.BlockSpec(memory_space=pltpu.VMEM),
        scratch_shapes=[
            pltpu.VMEM(dense.shape, dense.dtype),
            pltpu.VMEM((n_occ, n_vir, rows, width), jnp.bfloat16),
            pltpu.VMEM((n_occ, width // CUT, rows, CUT), jnp.float32),
            pltpu.VMEM((2, width // CUT, rows, CUT), jnp.float32),
            pltpu.VMEM((width // CUT, rows, CUT), jnp.float32),
            pltpu.SemaphoreType.DMA((N_SEM,)),
            pltpu.SemaphoreType.DMA((N_SEM,)),
            pltpu.SemaphoreType.DMA(()),
        ],
        compiler_params=pltpu.CompilerParams(
            collective_id=0, has_side_effects=True, vmem_limit_bytes=48 << 20
        ),
        name="ladder",
    )(amplitudes, dense)


def per_device(amplitudes, ladder_tiles, block_list):
    everywhere = lax.axis_size("occ") * amplitudes.size * GROUP * 2
    fits = everywhere <= 16 << 20 and amplitudes.shape[1] == 3 * CUT
    if lax.axis_size("vir") == GROUP and lax.axis_size("occ") == 4 and fits:
        return tiles_stay(amplitudes, ladder_tiles, block_list)
    return tiles_travel(amplitudes, ladder_tiles, block_list)


def solution(mesh):
    return jax.shard_map(
        per_device,
        mesh=mesh,
        in_specs=(P("occ", "vir"), P(("occ", "vir"), None, None), P(("occ", "vir"), None)),
        out_specs=P("occ", "vir"),
        check_vma=False,
    )
```

```python
import jax
import jax.numpy as jnp
from jax import lax
from jax.experimental import pallas as pl
from jax.experimental.pallas import tpu as pltpu
from jax.sharding import PartitionSpec as P

TV = 128
GROUP = 8


def from_partner(block, axis, apart):
    count = lax.axis_size(axis)
    route = []
    for low in range(count):
        high = low | 1 << apart
        if high != low and high < count:
            route += [(low, high), (high, low)]
    return lax.ppermute(block, axis, route)


def collect_group(local_amps, vir_index):
    gathered = local_amps
    for bit_number in range(GROUP.bit_length() - 1):
        partner = from_partner(gathered, "vir", bit_number)
        is_low = vir_index >> bit_number & 1 == 0
        gathered = jnp.where(
            is_low,
            jnp.concatenate([gathered, partner], axis=1),
            jnp.concatenate([partner, gathered], axis=1),
        )
    return gathered


def ladder_block(group_amps, ladder_mats, block_pairs, vir_index, tiles_here):
    group_count = group_amps.shape[1] // TV
    first_tile = vir_index // GROUP * GROUP * tiles_here
    out_tile = block_pairs[:, 1] - vir_index * tiles_here
    in_tile = block_pairs[:, 0] - first_tile
    is_live = block_pairs[:, 1] >= 0
    pair_index = jnp.where(is_live, in_tile * tiles_here + out_tile, -1)
    slot_onehot = (
        pair_index[:, None] == jnp.arange(group_count * tiles_here, dtype=jnp.int32)[None, :]
    ).astype(jnp.bfloat16)
    placed = jnp.einsum(
        "sp,skn->pkn", slot_onehot, ladder_mats, preferred_element_type=jnp.float32
    ).astype(jnp.bfloat16)
    dense_weight = (
        placed.reshape(group_count, tiles_here, TV, TV)
        .transpose(0, 2, 1, 3)
        .reshape(group_count * TV, tiles_here * TV)
    )
    return jnp.dot(group_amps, dense_weight, preferred_element_type=jnp.float32)


def tiles_travel(amplitudes, ladder_tiles, block_list):
    tiles_here = amplitudes.shape[1] // TV
    vir_index = lax.axis_index("vir")
    all_tiles, all_pairs = (
        lax.all_gather(ladder_tiles, "occ", axis=0, tiled=True),
        lax.all_gather(block_list, "occ", axis=0, tiled=True),
    )
    group_amps = collect_group(amplitudes, vir_index)
    residual = ladder_block(group_amps, all_tiles, all_pairs, vir_index, tiles_here).astype(
        jnp.bfloat16
    )
    return residual


def place_body(in_ref, out_ref, tiles_ref, dense_ref):
    def clear(k, carry):
        rows = pl.ds(pl.multiple_of(k * TV, TV), TV)
        dense_ref[rows, :] = jnp.zeros((TV, dense_ref.shape[1]), dense_ref.dtype)
        return carry

    lax.fori_loop(0, dense_ref.shape[0] // TV, clear, 0)

    def put(slot, carry):
        @pl.when(out_ref[slot] >= 0)
        def _():
            rows = pl.ds(pl.multiple_of(in_ref[slot] * TV, TV), TV)
            cols = pl.ds(pl.multiple_of(out_ref[slot] * TV, TV), TV)
            dense_ref[rows, cols] = tiles_ref[slot]

        return carry

    lax.fori_loop(0, tiles_ref.shape[0], put, 0)


def place_tiles(ladder_tiles, block_pairs, tiles_here):
    vir_index = lax.axis_index("vir")
    is_live = block_pairs[:, 1] >= 0
    in_tile = block_pairs[:, 0] - vir_index // GROUP * GROUP * tiles_here
    out_tile = block_pairs[:, 1] - vir_index * tiles_here
    in_tile = jnp.where(is_live, jnp.clip(in_tile, 0, GROUP * tiles_here - 1), 0)
    out_tile = jnp.where(is_live, jnp.clip(out_tile, 0, tiles_here - 1), -1)
    return pl.pallas_call(
        place_body,
        out_shape=jax.ShapeDtypeStruct((GROUP * tiles_here * TV, tiles_here * TV), ladder_tiles.dtype),
        in_specs=[
            pl.BlockSpec(memory_space=pltpu.SMEM),
            pl.BlockSpec(memory_space=pltpu.SMEM),
            pl.BlockSpec(memory_space=pltpu.VMEM),
        ],
        out_specs=pl.BlockSpec(memory_space=pltpu.VMEM),
        compiler_params=pltpu.CompilerParams(vmem_limit_bytes=32 << 20),
        cost_estimate=pl.CostEstimate(flops=0, bytes_accessed=24 << 20, transcendentals=0),
        name="place_tiles",
    )(in_tile, out_tile, ladder_tiles)


N_SEM = 57
CUT = 256


def ladder_body(
    amps_ref, dense_hbm, out_ref, dense_ref, all_ref, part, near, far, send_sems, recv_sems, dense_sem
):
    o, v = lax.axis_index("occ"), lax.axis_index("vir")
    y, x, c = v // 4, v // 2 % 2, v % 2
    v_x = y * 4 + (1 - x) * 2 + c
    v_y = (1 - y) * 4 + x * 2 + c
    v_xy = (1 - y) * 4 + (1 - x) * 2 + c
    v_c = y * 4 + x * 2 + 1 - c
    o_1 = o + 1 - 2 * (o % 2)
    o_of = (o, o_1, (o + 2) % 4, (o_1 + 2) % 4)
    rows, width = amps_ref.shape
    half = rows // 2
    whole, top, low = pl.ds(0, rows), pl.ds(0, half), pl.ds(half, half)

    barrier = pltpu.get_barrier_semaphore()
    peers = [(o_of[1], v), (o_of[2], v), (o_of[3], v), (o, v_x), (o, v_y), (o, v_c)]
    for peer in peers:
        pl.semaphore_signal(barrier, inc=1, device_id=peer, device_id_type=pl.DeviceIdType.MESH)
    all_ref[o, v] = amps_ref[...]
    pl.semaphore_wait(barrier, len(peers))

    started = []

    def move(src, dst, number, peer):
        copy = pltpu.make_async_remote_copy(
            src_ref=src,
            dst_ref=dst,
            send_sem=send_sems.at[number],
            recv_sem=recv_sems.at[number],
            device_id=peer,
            device_id_type=pl.DeviceIdType.MESH,
        )
        return copy

    def send(block, tile, span, number, peer):
        ref = all_ref.at[block, tile, span]
        copy = move(ref, ref, number, peer)
        copy.start()
        started.append(copy)

    def arrived(block, tile, span, number, peer):
        ref = all_ref.at[block, tile, span]
        move(ref, ref, number, peer).wait_recv()

    fetch = pltpu.make_async_copy(dense_hbm, dense_ref, dense_sem)
    fetch.start()

    def row_stage(e):
        send(o, v, whole, e, (o_of[e], v))

    def own_stage(e):
        block, base = o_of[e], 4 + 11 * e
        if e > 0:
            arrived(block, v, whole, e, (block, v))
        send(block, v, top, base, (o, v_x))
        send(block, v, low, base + 1, (o, v_y))
        send(block, v, low, base + 2, (o, v_x))
        send(block, v, top, base + 3, (o, v_y))
        send(block, v, whole, base + 6, (o, v_c))

    def forward_stage(e):
        block, base = o_of[e], 4 + 11 * e
        arrived(block, v_x, top, base, (o, v_x))
        send(block, v_x, top, base + 4, (o, v_y))
        arrived(block, v_y, low, base + 1, (o, v_y))
        send(block, v_y, low, base + 5, (o, v_x))
        arrived(block, v_x, low, base + 2, (o, v_x))
        send(block, v_x, whole, base + 7, (o, v_c))
        arrived(block, v_y, top, base + 3, (o, v_y))
        send(block, v_y, whole, base + 8, (o, v_c))

    def corner_stage(e):
        block, base = o_of[e], 4 + 11 * e
        arrived(block, v_xy, top, base + 4, (o, v_y))
        send(block, v_xy, top, base + 9, (o, v_c))
        arrived(block, v_xy, low, base + 5, (o, v_x))
        send(block, v_xy, low, base + 10, (o, v_c))

    def other_core(tile):
        return tile + 1 - 2 * c

    def product_stage(e):
        block, base = o_of[e], 4 + 11 * e
        arrived(block, other_core(v), whole, base + 6, (o, v_c))
        arrived(block, other_core(v_x), whole, base + 7, (o, v_c))
        arrived(block, other_core(v_y), whole, base + 8, (o, v_c))
        arrived(block, other_core(v_xy), top, base + 9, (o, v_c))
        arrived(block, other_core(v_xy), low, base + 10, (o, v_c))

        for n in range(width // CUT):
            columns = pl.ds(n * CUT, CUT)
            total = None
            for tile in range(GROUP):
                term = jnp.dot(
                    all_ref[block, tile],
                    dense_ref[pl.ds(tile * width, width), columns],
                    preferred_element_type=jnp.float32,
                )
                total = term if total is None else total + term
            part[e, n] = total
            if e == 1 or e == 3:
                slot = e // 2
                copy = move(part.at[e, n], near.at[slot, n], 48 + 3 * slot + n, (o_of[1], v))
                copy.start()
                started.append(copy)

    def far_stage():
        for n in range(width // CUT):
            move(part.at[2, n], near.at[1, n], 51 + n, (o_of[1], v)).wait_recv()
            part[2, n] += near[1, n]
            copy = move(part.at[2, n], far.at[n], 54 + n, (o_of[2], v))
            copy.start()
            started.append(copy)

    row_stage(3)
    own_stage(0)
    row_stage(2)
    forward_stage(0)
    corner_stage(0)
    own_stage(3)
    row_stage(1)
    forward_stage(3)
    own_stage(2)
    corner_stage(3)
    fetch.wait()
    product_stage(3)
    forward_stage(2)
    own_stage(1)
    corner_stage(2)
    product_stage(2)
    forward_stage(1)
    far_stage()
    corner_stage(1)
    product_stage(1)
    product_stage(0)
    for n in range(width // CUT):
        move(part.at[0, n], near.at[0, n], 48 + n, (o_of[1], v)).wait_recv()
        move(part.at[0, n], far.at[n], 54 + n, (o_of[2], v)).wait_recv()
        out_ref[:, pl.ds(n * CUT, CUT)] = (part[0, n] + near[0, n] + far[n]).astype(out_ref.dtype)
    for copy in started:
        copy.wait_send()


def tiles_stay(amplitudes, ladder_tiles, block_list):
    tiles_here = amplitudes.shape[1] // TV
    n_occ, n_vir = lax.axis_size("occ"), lax.axis_size("vir")
    dense = place_tiles(ladder_tiles, block_list, tiles_here)
    rows, width = amplitudes.shape
    return pl.pallas_call(
        ladder_body,
        out_shape=jax.ShapeDtypeStruct((rows, width), jnp.bfloat16),
        in_specs=[pl.BlockSpec(memory_space=pltpu.VMEM), pl.BlockSpec(memory_space=pl.ANY)],
        out_specs=pl.BlockSpec(memory_space=pltpu.VMEM),
        scratch_shapes=[
            pltpu.VMEM(dense.shape, dense.dtype),
            pltpu.VMEM((n_occ, n_vir, rows, width), jnp.bfloat16),
            pltpu.VMEM((n_occ, width // CUT, rows, CUT), jnp.float32),
            pltpu.VMEM((2, width // CUT, rows, CUT), jnp.float32),
            pltpu.VMEM((width // CUT, rows, CUT), jnp.float32),
            pltpu.SemaphoreType.DMA((N_SEM,)),
            pltpu.SemaphoreType.DMA((N_SEM,)),
            pltpu.SemaphoreType.DMA(()),
        ],
        compiler_params=pltpu.CompilerParams(
            collective_id=0, has_side_effects=True, vmem_limit_bytes=48 << 20
        ),
        name="ladder",
    )(amplitudes, dense)


def per_device(amplitudes, ladder_tiles, block_list):
    everywhere = lax.axis_size("occ") * amplitudes.size * GROUP * 2
    fits = everywhere <= 16 << 20 and amplitudes.shape[1] == 3 * CUT
    if lax.axis_size("vir") == GROUP and lax.axis_size("occ") == 4 and fits:
        return tiles_stay(amplitudes, ladder_tiles, block_list)
    return tiles_travel(amplitudes, ladder_tiles, block_list)


def solution(mesh):
    return jax.shard_map(
        per_device,
        mesh=mesh,
        in_specs=(P("occ", "vir"), P(("occ", "vir"), None, None), P(("occ", "vir"), None)),
        out_specs=P("occ", "vir"),
        check_vma=False,
    )
```

```python
import jax
import jax.numpy as jnp
from jax import lax
from jax.experimental import pallas as pl
from jax.experimental.pallas import tpu as pltpu
from jax.sharding import PartitionSpec as P

TV = 128
GROUP = 8


def from_partner(block, axis, apart):
    count = lax.axis_size(axis)
    route = []
    for low in range(count):
        high = low | 1 << apart
        if high != low and high < count:
            route += [(low, high), (high, low)]
    return lax.ppermute(block, axis, route)


def collect_group(local_amps, vir_index):
    gathered = local_amps
    for bit_number in range(GROUP.bit_length() - 1):
        partner = from_partner(gathered, "vir", bit_number)
        is_low = vir_index >> bit_number & 1 == 0
        gathered = jnp.where(
            is_low,
            jnp.concatenate([gathered, partner], axis=1),
            jnp.concatenate([partner, gathered], axis=1),
        )
    return gathered


def ladder_block(group_amps, ladder_mats, block_pairs, vir_index, tiles_here):
    group_count = group_amps.shape[1] // TV
    first_tile = vir_index // GROUP * GROUP * tiles_here
    out_tile = block_pairs[:, 1] - vir_index * tiles_here
    in_tile = block_pairs[:, 0] - first_tile
    is_live = block_pairs[:, 1] >= 0
    pair_index = jnp.where(is_live, in_tile * tiles_here + out_tile, -1)
    slot_onehot = (
        pair_index[:, None] == jnp.arange(group_count * tiles_here, dtype=jnp.int32)[None, :]
    ).astype(jnp.bfloat16)
    placed = jnp.einsum(
        "sp,skn->pkn", slot_onehot, ladder_mats, preferred_element_type=jnp.float32
    ).astype(jnp.bfloat16)
    dense_weight = (
        placed.reshape(group_count, tiles_here, TV, TV)
        .transpose(0, 2, 1, 3)
        .reshape(group_count * TV, tiles_here * TV)
    )
    return jnp.dot(group_amps, dense_weight, preferred_element_type=jnp.float32)


def tiles_travel(amplitudes, ladder_tiles, block_list):
    tiles_here = amplitudes.shape[1] // TV
    vir_index = lax.axis_index("vir")
    all_tiles, all_pairs = (
        lax.all_gather(ladder_tiles, "occ", axis=0, tiled=True),
        lax.all_gather(block_list, "occ", axis=0, tiled=True),
    )
    group_amps = collect_group(amplitudes, vir_index)
    residual = ladder_block(group_amps, all_tiles, all_pairs, vir_index, tiles_here).astype(
        jnp.bfloat16
    )
    return residual


def place_body(in_ref, out_ref, tiles_ref, dense_ref):
    def clear(k, carry):
        rows = pl.ds(pl.multiple_of(k * TV, TV), TV)
        dense_ref[rows, :] = jnp.zeros((TV, dense_ref.shape[1]), dense_ref.dtype)
        return carry

    lax.fori_loop(0, dense_ref.shape[0] // TV, clear, 0)

    def put(slot, carry):
        @pl.when(out_ref[slot] >= 0)
        def _():
            rows = pl.ds(pl.multiple_of(in_ref[slot] * TV, TV), TV)
            cols = pl.ds(pl.multiple_of(out_ref[slot] * TV, TV), TV)
            dense_ref[rows, cols] = tiles_ref[slot]

        return carry

    lax.fori_loop(0, tiles_ref.shape[0], put, 0)


def place_tiles(ladder_tiles, block_pairs, tiles_here):
    vir_index = lax.axis_index("vir")
    is_live = block_pairs[:, 1] >= 0
    in_tile = block_pairs[:, 0] - vir_index // GROUP * GROUP * tiles_here
    out_tile = block_pairs[:, 1] - vir_index * tiles_here
    in_tile = jnp.where(is_live, jnp.clip(in_tile, 0, GROUP * tiles_here - 1), 0)
    out_tile = jnp.where(is_live, jnp.clip(out_tile, 0, tiles_here - 1), -1)
    return pl.pallas_call(
        place_body,
        out_shape=jax.ShapeDtypeStruct((GROUP * tiles_here * TV, tiles_here * TV), ladder_tiles.dtype),
        in_specs=[
            pl.BlockSpec(memory_space=pltpu.SMEM),
            pl.BlockSpec(memory_space=pltpu.SMEM),
            pl.BlockSpec(memory_space=pltpu.VMEM),
        ],
        out_specs=pl.BlockSpec(memory_space=pltpu.VMEM),
        compiler_params=pltpu.CompilerParams(vmem_limit_bytes=32 << 20),
        cost_estimate=pl.CostEstimate(flops=0, bytes_accessed=24 << 20, transcendentals=0),
        name="place_tiles",
    )(in_tile, out_tile, ladder_tiles)


N_SEM = 114
CUT = 256


def ladder_body(
    amps_ref, dense_hbm, out_ref, dense_ref, all_ref, part, near, far, send_sems, recv_sems, dense_sem
):
    o, v = lax.axis_index("occ"), lax.axis_index("vir")
    y, x, c = v // 4, v // 2 % 2, v % 2
    v_x = y * 4 + (1 - x) * 2 + c
    v_y = (1 - y) * 4 + x * 2 + c
    v_xy = (1 - y) * 4 + (1 - x) * 2 + c
    v_c = y * 4 + x * 2 + 1 - c
    o_1 = o + 1 - 2 * (o % 2)
    o_of = (o, o_1, (o + 2) % 4, (o_1 + 2) % 4)
    rows, width = amps_ref.shape
    half, quarter = rows // 2, rows // 4
    whole = tuple(pl.ds(r * half, half) for r in range(2))
    top = tuple(pl.ds(r * half, quarter) for r in range(2))
    low = tuple(pl.ds(r * half + quarter, quarter) for r in range(2))

    barrier = pltpu.get_barrier_semaphore()
    peers = [(o_of[1], v), (o_of[2], v), (o_of[3], v), (o, v_x), (o, v_y), (o, v_c)]
    for peer in peers:
        pl.semaphore_signal(barrier, inc=1, device_id=peer, device_id_type=pl.DeviceIdType.MESH)
    all_ref[o, v] = amps_ref[...]
    pl.semaphore_wait(barrier, len(peers))

    started = []

    def move(src, dst, number, peer):
        copy = pltpu.make_async_remote_copy(
            src_ref=src,
            dst_ref=dst,
            send_sem=send_sems.at[number],
            recv_sem=recv_sems.at[number],
            device_id=peer,
            device_id_type=pl.DeviceIdType.MESH,
        )
        return copy

    def send(block, tile, span, number, peer):
        ref = all_ref.at[block, tile, span]
        copy = move(ref, ref, number, peer)
        copy.start()
        started.append(copy)

    def arrived(block, tile, span, number, peer):
        ref = all_ref.at[block, tile, span]
        move(ref, ref, number, peer).wait_recv()

    fetch = pltpu.make_async_copy(dense_hbm, dense_ref, dense_sem)
    fetch.start()

    def row_stage(e, r):
        send(o, v, whole[r], 2 * e + r, (o_of[e], v))

    def own_stage(e, r):
        block, base = o_of[e], 8 + 11 * (2 * e + r)
        if e > 0:
            arrived(block, v, whole[r], 2 * e + r, (block, v))
        send(block, v, top[r], base, (o, v_x))
        send(block, v, low[r], base + 1, (o, v_y))
        send(block, v, low[r], base + 2, (o, v_x))
        send(block, v, top[r], base + 3, (o, v_y))
        send(block, v, whole[r], base + 6, (o, v_c))

    def forward_stage(e, r):
        block, base = o_of[e], 8 + 11 * (2 * e + r)
        arrived(block, v_x, top[r], base, (o, v_x))
        send(block, v_x, top[r], base + 4, (o, v_y))
        arrived(block, v_y, low[r], base + 1, (o, v_y))
        send(block, v_y, low[r], base + 5, (o, v_x))
        arrived(block, v_x, low[r], base + 2, (o, v_x))
        send(block, v_x, whole[r], base + 7, (o, v_c))
        arrived(block, v_y, top[r], base + 3, (o, v_y))
        send(block, v_y, whole[r], base + 8, (o, v_c))

    def corner_stage(e, r):
        block, base = o_of[e], 8 + 11 * (2 * e + r)
        arrived(block, v_xy, top[r], base + 4, (o, v_y))
        send(block, v_xy, top[r], base + 9, (o, v_c))
        arrived(block, v_xy, low[r], base + 5, (o, v_x))
        send(block, v_xy, low[r], base + 10, (o, v_c))

    def other_core(tile):
        return tile + 1 - 2 * c

    def product_stage(e, r):
        block, base = o_of[e], 8 + 11 * (2 * e + r)
        arrived(block, other_core(v), whole[r], base + 6, (o, v_c))
        arrived(block, other_core(v_x), whole[r], base + 7, (o, v_c))
        arrived(block, other_core(v_y), whole[r], base + 8, (o, v_c))
        arrived(block, other_core(v_xy), top[r], base + 9, (o, v_c))
        arrived(block, other_core(v_xy), low[r], base + 10, (o, v_c))

        for n in range(width // CUT):
            columns = pl.ds(n * CUT, CUT)
            total = None
            for tile in range(GROUP):
                term = jnp.dot(
                    all_ref[block, tile, whole[r]],
                    dense_ref[pl.ds(tile * width, width), columns],
                    preferred_element_type=jnp.float32,
                )
                total = term if total is None else total + term
            part[e, r, n] = total
            if e == 1 or e == 3:
                slot = e // 2
                copy = move(part.at[e, r, n], near.at[slot, r, n], 96 + 6 * slot + 3 * r + n, (o_of[1], v))
                copy.start()
                started.append(copy)

    def far_stage(r):
        for n in range(width // CUT):
            move(part.at[2, r, n], near.at[1, r, n], 102 + 3 * r + n, (o_of[1], v)).wait_recv()
            part[2, r, n] += near[1, r, n]
            copy = move(part.at[2, r, n], far.at[r, n], 108 + 3 * r + n, (o_of[2], v))
            copy.start()
            started.append(copy)

    row_stage(3, 0)
    own_stage(0, 0)
    own_stage(0, 1)
    row_stage(2, 0)
    forward_stage(0, 0)
    row_stage(3, 1)
    forward_stage(0, 1)
    own_stage(3, 0)
    row_stage(2, 1)
    corner_stage(0, 0)
    corner_stage(0, 1)
    forward_stage(3, 0)
    own_stage(2, 0)
    row_stage(1, 0)
    row_stage(1, 1)
    corner_stage(3, 0)
    own_stage(3, 1)
    fetch.wait()
    product_stage(3, 0)
    forward_stage(2, 0)
    own_stage(2, 1)
    corner_stage(2, 0)
    forward_stage(3, 1)
    product_stage(2, 0)
    corner_stage(3, 1)
    far_stage(0)
    product_stage(3, 1)
    forward_stage(2, 1)
    own_stage(1, 0)
    own_stage(1, 1)
    corner_stage(2, 1)
    product_stage(2, 1)
    forward_stage(1, 0)
    far_stage(1)
    forward_stage(1, 1)
    corner_stage(1, 0)
    product_stage(1, 0)
    corner_stage(1, 1)
    product_stage(1, 1)
    product_stage(0, 0)
    product_stage(0, 1)
    for r in range(2):
        for n in range(width // CUT):
            move(part.at[0, r, n], near.at[0, r, n], 96 + 3 * r + n, (o_of[1], v)).wait_recv()
            move(part.at[0, r, n], far.at[r, n], 108 + 3 * r + n, (o_of[2], v)).wait_recv()
            out_ref[whole[r], pl.ds(n * CUT, CUT)] = (
                part[0, r, n] + near[0, r, n] + far[r, n]
            ).astype(out_ref.dtype)
    for copy in started:
        copy.wait_send()


def tiles_stay(amplitudes, ladder_tiles, block_list):
    tiles_here = amplitudes.shape[1] // TV
    n_occ, n_vir = lax.axis_size("occ"), lax.axis_size("vir")
    dense = place_tiles(ladder_tiles, block_list, tiles_here)
    rows, width = amplitudes.shape
    return pl.pallas_call(
        ladder_body,
        out_shape=jax.ShapeDtypeStruct((rows, width), jnp.bfloat16),
        in_specs=[pl.BlockSpec(memory_space=pltpu.VMEM), pl.BlockSpec(memory_space=pl.ANY)],
        out_specs=pl.BlockSpec(memory_space=pltpu.VMEM),
        scratch_shapes=[
            pltpu.VMEM(dense.shape, dense.dtype),
            pltpu.VMEM((n_occ, n_vir, rows, width), jnp.bfloat16),
            pltpu.VMEM((n_occ, 2, width // CUT, rows // 2, CUT), jnp.float32),
            pltpu.VMEM((2, 2, width // CUT, rows // 2, CUT), jnp.float32),
            pltpu.VMEM((2, width // CUT, rows // 2, CUT), jnp.float32),
            pltpu.SemaphoreType.DMA((N_SEM,)),
            pltpu.SemaphoreType.DMA((N_SEM,)),
            pltpu.SemaphoreType.DMA(()),
        ],
        compiler_params=pltpu.CompilerParams(
            collective_id=0, has_side_effects=True, vmem_limit_bytes=48 << 20
        ),
        name="ladder",
    )(amplitudes, dense)


def per_device(amplitudes, ladder_tiles, block_list):
    everywhere = lax.axis_size("occ") * amplitudes.size * GROUP * 2
    even = amplitudes.shape[0] % 64 == 0 and amplitudes.shape[1] % CUT == 0
    fits = everywhere <= 16 << 20 and even
    if lax.axis_size("vir") == GROUP and lax.axis_size("occ") == 4 and fits:
        return tiles_stay(amplitudes, ladder_tiles, block_list)
    return tiles_travel(amplitudes, ladder_tiles, block_list)


def solution(mesh):
    return jax.shard_map(
        per_device,
        mesh=mesh,
        in_specs=(P("occ", "vir"), P(("occ", "vir"), None, None), P(("occ", "vir"), None)),
        out_specs=P("occ", "vir"),
        check_vma=False,
    )
```

```python
import jax
import jax.numpy as jnp
from jax import lax
from jax.experimental import pallas as pl
from jax.experimental.pallas import tpu as pltpu
from jax.sharding import PartitionSpec as P

TV = 128
GROUP = 8


def from_partner(block, axis, apart):
    count = lax.axis_size(axis)
    route = []
    for low in range(count):
        high = low | 1 << apart
        if high != low and high < count:
            route += [(low, high), (high, low)]
    return lax.ppermute(block, axis, route)


def collect_group(local_amps, vir_index):
    gathered = local_amps
    for bit_number in range(GROUP.bit_length() - 1):
        partner = from_partner(gathered, "vir", bit_number)
        is_low = vir_index >> bit_number & 1 == 0
        gathered = jnp.where(
            is_low,
            jnp.concatenate([gathered, partner], axis=1),
            jnp.concatenate([partner, gathered], axis=1),
        )
    return gathered


def ladder_block(group_amps, ladder_mats, block_pairs, vir_index, tiles_here):
    group_count = group_amps.shape[1] // TV
    first_tile = vir_index // GROUP * GROUP * tiles_here
    out_tile = block_pairs[:, 1] - vir_index * tiles_here
    in_tile = block_pairs[:, 0] - first_tile
    is_live = block_pairs[:, 1] >= 0
    pair_index = jnp.where(is_live, in_tile * tiles_here + out_tile, -1)
    slot_onehot = (
        pair_index[:, None] == jnp.arange(group_count * tiles_here, dtype=jnp.int32)[None, :]
    ).astype(jnp.bfloat16)
    placed = jnp.einsum(
        "sp,skn->pkn", slot_onehot, ladder_mats, preferred_element_type=jnp.float32
    ).astype(jnp.bfloat16)
    dense_weight = (
        placed.reshape(group_count, tiles_here, TV, TV)
        .transpose(0, 2, 1, 3)
        .reshape(group_count * TV, tiles_here * TV)
    )
    return jnp.dot(group_amps, dense_weight, preferred_element_type=jnp.float32)


def tiles_travel(amplitudes, ladder_tiles, block_list):
    tiles_here = amplitudes.shape[1] // TV
    vir_index = lax.axis_index("vir")
    all_tiles, all_pairs = (
        lax.all_gather(ladder_tiles, "occ", axis=0, tiled=True),
        lax.all_gather(block_list, "occ", axis=0, tiled=True),
    )
    group_amps = collect_group(amplitudes, vir_index)
    residual = ladder_block(group_amps, all_tiles, all_pairs, vir_index, tiles_here).astype(
        jnp.bfloat16
    )
    return residual


def place_body(in_ref, out_ref, tiles_ref, dense_ref):
    def clear(k, carry):
        rows = pl.ds(pl.multiple_of(k * TV, TV), TV)
        dense_ref[rows, :] = jnp.zeros((TV, dense_ref.shape[1]), dense_ref.dtype)
        return carry

    lax.fori_loop(0, dense_ref.shape[0] // TV, clear, 0)

    def put(slot, carry):
        @pl.when(out_ref[slot] >= 0)
        def _():
            rows = pl.ds(pl.multiple_of(in_ref[slot] * TV, TV), TV)
            cols = pl.ds(pl.multiple_of(out_ref[slot] * TV, TV), TV)
            dense_ref[rows, cols] = tiles_ref[slot]

        return carry

    lax.fori_loop(0, tiles_ref.shape[0], put, 0)


def place_tiles(ladder_tiles, block_pairs, tiles_here):
    vir_index = lax.axis_index("vir")
    is_live = block_pairs[:, 1] >= 0
    in_tile = block_pairs[:, 0] - vir_index // GROUP * GROUP * tiles_here
    out_tile = block_pairs[:, 1] - vir_index * tiles_here
    in_tile = jnp.where(is_live, jnp.clip(in_tile, 0, GROUP * tiles_here - 1), 0)
    out_tile = jnp.where(is_live, jnp.clip(out_tile, 0, tiles_here - 1), -1)
    return pl.pallas_call(
        place_body,
        out_shape=jax.ShapeDtypeStruct((GROUP * tiles_here * TV, tiles_here * TV), ladder_tiles.dtype),
        in_specs=[
            pl.BlockSpec(memory_space=pltpu.SMEM),
            pl.BlockSpec(memory_space=pltpu.SMEM),
            pl.BlockSpec(memory_space=pltpu.VMEM),
        ],
        out_specs=pl.BlockSpec(memory_space=pltpu.VMEM),
        compiler_params=pltpu.CompilerParams(vmem_limit_bytes=32 << 20),
        cost_estimate=pl.CostEstimate(flops=0, bytes_accessed=24 << 20, transcendentals=0),
        name="place_tiles",
    )(in_tile, out_tile, ladder_tiles)


N_SEM = 114
CUT = 256


def ladder_body(
    amps_ref, dense_hbm, out_ref, dense_ref, all_ref, part, near, far, send_sems, recv_sems, dense_sem
):
    o, v = lax.axis_index("occ"), lax.axis_index("vir")
    y, x, c = v // 4, v // 2 % 2, v % 2
    v_x = y * 4 + (1 - x) * 2 + c
    v_y = (1 - y) * 4 + x * 2 + c
    v_xy = (1 - y) * 4 + (1 - x) * 2 + c
    v_c = y * 4 + x * 2 + 1 - c
    o_1 = o + 1 - 2 * (o % 2)
    o_of = (o, o_1, (o + 2) % 4, (o_1 + 2) % 4)
    rows, width = amps_ref.shape
    half, quarter = rows // 2, rows // 4
    whole = tuple(pl.ds(r * half, half) for r in range(2))
    top = tuple(pl.ds(r * half, quarter) for r in range(2))
    low = tuple(pl.ds(r * half + quarter, quarter) for r in range(2))

    barrier = pltpu.get_barrier_semaphore()
    peers = [(o_of[1], v), (o_of[2], v), (o_of[3], v), (o, v_x), (o, v_y), (o, v_c)]
    for peer in peers:
        pl.semaphore_signal(barrier, inc=1, device_id=peer, device_id_type=pl.DeviceIdType.MESH)
    all_ref[o, v] = amps_ref[...]
    pl.semaphore_wait(barrier, len(peers))

    started = []

    def move(src, dst, number, peer):
        copy = pltpu.make_async_remote_copy(
            src_ref=src,
            dst_ref=dst,
            send_sem=send_sems.at[number],
            recv_sem=recv_sems.at[number],
            device_id=peer,
            device_id_type=pl.DeviceIdType.MESH,
        )
        return copy

    def send(block, tile, span, number, peer):
        ref = all_ref.at[block, tile, span]
        copy = move(ref, ref, number, peer)
        copy.start()
        started.append(copy)

    def arrived(block, tile, span, number, peer):
        ref = all_ref.at[block, tile, span]
        move(ref, ref, number, peer).wait_recv()

    fetch = pltpu.make_async_copy(dense_hbm, dense_ref, dense_sem)
    fetch.start()

    def row_stage(e, r):
        send(o, v, whole[r], 2 * e + r, (o_of[e], v))

    def own_stage(e, r):
        block, base = o_of[e], 8 + 11 * (2 * e + r)
        if e > 0:
            arrived(block, v, whole[r], 2 * e + r, (block, v))
        send(block, v, top[r], base, (o, v_x))
        send(block, v, low[r], base + 1, (o, v_y))
        send(block, v, low[r], base + 2, (o, v_x))
        send(block, v, top[r], base + 3, (o, v_y))
        send(block, v, whole[r], base + 6, (o, v_c))

    def forward_stage(e, r):
        block, base = o_of[e], 8 + 11 * (2 * e + r)
        arrived(block, v_x, top[r], base, (o, v_x))
        send(block, v_x, top[r], base + 4, (o, v_y))
        arrived(block, v_y, low[r], base + 1, (o, v_y))
        send(block, v_y, low[r], base + 5, (o, v_x))
        arrived(block, v_x, low[r], base + 2, (o, v_x))
        send(block, v_x, whole[r], base + 7, (o, v_c))
        arrived(block, v_y, top[r], base + 3, (o, v_y))
        send(block, v_y, whole[r], base + 8, (o, v_c))

    def corner_stage(e, r):
        block, base = o_of[e], 8 + 11 * (2 * e + r)
        arrived(block, v_xy, top[r], base + 4, (o, v_y))
        send(block, v_xy, top[r], base + 9, (o, v_c))
        arrived(block, v_xy, low[r], base + 5, (o, v_x))
        send(block, v_xy, low[r], base + 10, (o, v_c))

    def other_core(tile):
        return tile + 1 - 2 * c

    def product_stage(e, r):
        block, base = o_of[e], 8 + 11 * (2 * e + r)
        arrived(block, other_core(v), whole[r], base + 6, (o, v_c))
        arrived(block, other_core(v_x), whole[r], base + 7, (o, v_c))
        arrived(block, other_core(v_y), whole[r], base + 8, (o, v_c))
        arrived(block, other_core(v_xy), top[r], base + 9, (o, v_c))
        arrived(block, other_core(v_xy), low[r], base + 10, (o, v_c))

        for n in range(width // CUT):
            columns = pl.ds(n * CUT, CUT)
            total = None
            for tile in range(GROUP):
                term = jnp.dot(
                    all_ref[block, tile, whole[r]],
                    dense_ref[pl.ds(tile * width, width), columns],
                    preferred_element_type=jnp.float32,
                )
                total = term if total is None else total + term
            part[e, r, n] = total
            if e == 1 or e == 3:
                slot = e // 2
                copy = move(part.at[e, r, n], near.at[slot, r, n], 96 + 6 * slot + 3 * r + n, (o_of[1], v))
                copy.start()
                started.append(copy)

    def far_stage(r):
        for n in range(width // CUT):
            move(part.at[2, r, n], near.at[1, r, n], 102 + 3 * r + n, (o_of[1], v)).wait_recv()
            part[2, r, n] += near[1, r, n]
            copy = move(part.at[2, r, n], far.at[r, n], 108 + 3 * r + n, (o_of[2], v))
            copy.start()
            started.append(copy)

    row_stage(3, 0)
    own_stage(0, 0)
    own_stage(0, 1)
    row_stage(2, 0)
    forward_stage(0, 0)
    row_stage(3, 1)
    forward_stage(0, 1)
    own_stage(3, 0)
    row_stage(2, 1)
    corner_stage(0, 0)
    corner_stage(0, 1)
    forward_stage(3, 0)
    own_stage(2, 0)
    row_stage(1, 0)
    row_stage(1, 1)
    corner_stage(3, 0)
    own_stage(3, 1)
    fetch.wait()
    product_stage(3, 0)
    forward_stage(2, 0)
    own_stage(2, 1)
    corner_stage(2, 0)
    forward_stage(3, 1)
    product_stage(2, 0)
    corner_stage(3, 1)
    far_stage(0)
    product_stage(3, 1)
    forward_stage(2, 1)
    own_stage(1, 0)
    own_stage(1, 1)
    corner_stage(2, 1)
    product_stage(2, 1)
    forward_stage(1, 0)
    far_stage(1)
    forward_stage(1, 1)
    corner_stage(1, 0)
    product_stage(1, 0)
    corner_stage(1, 1)
    product_stage(1, 1)
    product_stage(0, 0)
    product_stage(0, 1)
    for r in range(2):
        for n in range(width // CUT):
            move(part.at[0, r, n], near.at[0, r, n], 96 + 3 * r + n, (o_of[1], v)).wait_recv()
            move(part.at[0, r, n], far.at[r, n], 108 + 3 * r + n, (o_of[2], v)).wait_recv()
            out_ref[whole[r], pl.ds(n * CUT, CUT)] = (
                part[0, r, n] + near[0, r, n] + far[r, n]
            ).astype(out_ref.dtype)
    for copy in started:
        copy.wait_send()


def tiles_stay(amplitudes, ladder_tiles, block_list):
    tiles_here = amplitudes.shape[1] // TV
    n_occ, n_vir = lax.axis_size("occ"), lax.axis_size("vir")
    dense = place_tiles(ladder_tiles, block_list, tiles_here)
    rows, width = amplitudes.shape
    return pl.pallas_call(
        ladder_body,
        out_shape=jax.ShapeDtypeStruct((rows, width), jnp.bfloat16),
        in_specs=[pl.BlockSpec(memory_space=pltpu.VMEM), pl.BlockSpec(memory_space=pl.ANY)],
        out_specs=pl.BlockSpec(memory_space=pltpu.VMEM),
        scratch_shapes=[
            pltpu.VMEM(dense.shape, dense.dtype),
            pltpu.VMEM((n_occ, n_vir, rows, width), jnp.bfloat16),
            pltpu.VMEM((n_occ, 2, width // CUT, rows // 2, CUT), jnp.float32),
            pltpu.VMEM((2, 2, width // CUT, rows // 2, CUT), jnp.float32),
            pltpu.VMEM((2, width // CUT, rows // 2, CUT), jnp.float32),
            pltpu.SemaphoreType.DMA((N_SEM,)),
            pltpu.SemaphoreType.DMA((N_SEM,)),
            pltpu.SemaphoreType.DMA(()),
        ],
        compiler_params=pltpu.CompilerParams(
            collective_id=0, has_side_effects=True, vmem_limit_bytes=40 << 20
        ),
        name="ladder",
    )(amplitudes, dense)


def per_device(amplitudes, ladder_tiles, block_list):
    everywhere = lax.axis_size("occ") * amplitudes.size * GROUP * 2
    even = amplitudes.shape[0] % 64 == 0 and amplitudes.shape[1] % CUT == 0
    fits = everywhere <= 16 << 20 and even
    if lax.axis_size("vir") == GROUP and lax.axis_size("occ") == 4 and fits:
        return tiles_stay(amplitudes, ladder_tiles, block_list)
    return tiles_travel(amplitudes, ladder_tiles, block_list)


def solution(mesh):
    return jax.shard_map(
        per_device,
        mesh=mesh,
        in_specs=(P("occ", "vir"), P(("occ", "vir"), None, None), P(("occ", "vir"), None)),
        out_specs=P("occ", "vir"),
        check_vma=False,
    )
```
